128 devices in a mesh: ja: 32 (over x_hi, z, y), ia: 4 (over x_lo, core).
Axes of the slice: x: 4 (x_hi: 2, x_lo: 2; x = x_hi * 2 + x_lo), y: 4, z: 4, core: 2. Of those that a mesh axis runs over, the one named last changes fastest.
Arguments:
- argo_value: float32 [131072, 150], P(('ja', 'ia')), may hold values from -6 to 6
- argo_owner: int32 [131072, 1], P(('ja', 'ia')), may hold values from 0 to 127; in each aligned block of 1024 rows (0 to 1023, 1024 to 2047, ...) at most 24 rows name the same one
- argo_cell: int32 [131072], P(('ja', 'ia')), may hold values from 0 to 8191
- alt_value: float32 [98304], P(('ja', 'ia')), may hold values from -6 to 6
- alt_owner: int32 [98304, 1], P(('ja', 'ia')), may hold values from 0 to 127; in each aligned block of 768 rows (0 to 767, 768 to 1535, ...) at most 18 rows name the same one
- alt_cell: int32 [98304], P(('ja', 'ia')), may hold values from 0 to 8191
- alt_profile: float32 [150], replicated, may hold values from -3 to 3
- land_mask: int32 [512, 2048], P('ja', 'ia'), may hold values 0 or 1
- coef_east: float32 [512, 2048], P('ja', 'ia'), may hold values from 0.05 to 0.24
- coef_north: float32 [512, 2048], P('ja', 'ia'), may hold values from 0.05 to 0.24
- mirror: int32 [2048], P('ia'), may hold values from 0 to 2047, as said below
- vinv: float32 [512, 2, 75, 75], P('ja'), may hold values from -1 to 1
Outputs:
- gradient: float32 [150, 512, 2048], P(None, 'ja', 'ia')
The draws below stay inside these ranges and needn't reach their ends.
Inputs may be any that keep to these rules, and one draw needn't show every extreme that they name: `argo_owner`: the rows of one device name one owner at most 24 times, a bound that some block reaches. `alt_owner`: the rows of one device name one owner at most 18 times, a bound that some block reaches. mirror[i] is 2047 - i or 2047 - (i XOR 1), and mirror[mirror[i]] = i.
All inputs are finite; a program needn't handle non-finite values. No bound on the sum of `land_mask` on one device may be relied on, other than what follows from the above.
Results may differ from the reference program's by a relative error of at most 0.0001.
Values sent between devices are 32-bit elements; how exact they have to be, the bound alone decides.
A program may use at most 128 MiB of HBM per device.

```python
import math
import jax
import jax.numpy as jnp
import numpy as np
from jax import lax

K = 75
CJ = 16
CI = 512
OBS_DEV = 1024
ALT_DEV = 768
ITERS = 3
NJ = 512
NI = 2048
TOTAL_OBS = 131072
TOTAL_ALT = 98304
CAP = 24
CAPH = 18
N_IA = 4
DEVICES = 128


def draw_mirror(key, part):
    half_count = NI // 2
    flip_bits = jax.random.randint(key, (NI // 4,), 0, 2, dtype=jnp.int32)
    lower_half = jnp.arange(half_count, dtype=jnp.int32)
    lower_map = NI - 1 - jnp.bitwise_xor(lower_half, flip_bits[lower_half // 2])
    upper_half = jnp.arange(half_count, NI, dtype=jnp.int32)
    mirrored = NI - 1 - upper_half
    upper_map = jnp.bitwise_xor(mirrored, flip_bits[mirrored // 2])
    return jnp.concatenate([lower_map, upper_map]).astype(jnp.int32)


def draw_vinv(key, part):
    first_key, second_key = jax.random.split(jax.random.fold_in(key, 17))
    off_part = jnp.clip(jax.random.normal(first_key, (NJ, 2, K, K), jnp.float32), -4.0, 4.0) * (0.35 / K ** 0.5)
    diag_part = jax.random.uniform(second_key, (NJ, 2, K, 1), jnp.float32, 0.5, 1.0)
    identity = (jnp.arange(K)[:, None] == jnp.arange(K)[None, :]).astype(jnp.float32)
    return (off_part * (1.0 - identity) + diag_part * identity).astype(jnp.float32)


def plant(entries, key, least, largest):
    dims = entries.shape
    place = [jax.random.randint(jax.random.fold_in(key, axis), (), 0, dims[axis]) for axis in range(len(dims))]
    entries = entries.at[tuple(place)].set(least)
    longest = dims.index(max(dims))
    place[longest] = (place[longest] + 1) % dims[longest]
    return entries.at[tuple(place)].set(largest)


def levels(key, extent, shards, low, top_value):
    gain = 1.0
    for position, shards_of in shards:
        steps = jax.random.uniform(jax.random.fold_in(jax.random.fold_in(key, 6), position), (shards_of,), jnp.float32, low / len(shards), top_value / len(shards))
        gain = gain * jnp.repeat(jnp.exp(steps), extent[position] // shards_of).reshape((-1,) + (1,) * (len(extent) - 1 - position))
    return gain


def assign_block(key, own, number, rows, count, top, limit, slope):
    sequence = jax.random.permutation(key, count)
    crowded, ordinary = portions_of(count, rows * top, limit, slope, True), portions_of(count, rows * top, limit, slope, False)
    places = jnp.arange(count)

    def named(lengths, offset_by):
        used = int((lengths > 0).sum())
        fixed = max(1, used // 4)
        moved = fixed + (places - fixed + offset_by * (used - fixed)) % max(1, count - fixed)
        return jnp.zeros((count,), jnp.int32).at[sequence[jnp.where(places < fixed, places, moved)]].set(jnp.asarray(lengths, jnp.int32))

    lengths = jnp.where(number % 4 == 0, named(crowded, number // 4), named(ordinary, number - number // 4 - 1))
    mixed = jax.random.permutation(jax.random.fold_in(own, 3), count)
    donor, sink = mixed[0:count // 2 * 2:2], mixed[1:count // 2 * 2:2]
    room = jnp.minimum(lengths[donor] - 1, limit - lengths[sink]) // 2
    room = jnp.where((donor == sequence[0]) | (sink == sequence[0]) | (lengths[sink] == 0), 0, jnp.maximum(room, 0))
    moved = jax.random.randint(jax.random.fold_in(own, 4), (count // 2,), 0, 1 << 20) % (room + 1)
    lengths = lengths.at[donor].add(-moved).at[sink].add(moved)
    items = jnp.searchsorted(jnp.cumsum(lengths), jnp.arange(rows * top), side="right").astype(jnp.int32)
    listing = items.reshape(top, rows).T
    listing = listing[jax.random.permutation(jax.random.fold_in(own, 1), rows)]
    offset_by = jax.random.randint(jax.random.fold_in(own, 2), (rows, 1), 0, top)
    return jnp.take_along_axis(listing, (jnp.arange(top)[None, :] + offset_by) % top, axis=1)


def portions_of(count, total, most, slope, full):
    weights = [(1 << 20) // math.isqrt(standing ** slope) + 1 for standing in range(1, count + 1)]
    largest = most if full else min(most, max(-(-total // count), total * weights[0] // sum(weights)))
    least = 1 if total - largest >= count - 1 else 0
    given, spare = [largest] + [least] * (count - 1), total - largest - least * (count - 1)
    while spare > 0:
        free = [i for i in range(1, count) if given[i] < largest] or [i for i in range(1, count) if given[i] < most]
        mass, left = sum([weights[i] for i in free]), spare
        for i in free:
            addition = min(most - given[i], max(1, left * weights[i] // mass), spare)
            given[i] = given[i] + addition
            spare = spare - addition
    return np.array(given)


def normal_values(own_key, extent, spread, bound, cuts=(), kind=jnp.bfloat16):
    level = levels(own_key, extent, cuts, -0.22, 0.18) if cuts else 1.0
    values = jax.random.normal(own_key, extent, jnp.float32) * spread * level
    return jnp.minimum(jnp.maximum(values, -bound), bound).astype(kind)


def setup_inputs(seed: int = 0) -> dict:
    keys = jax.random.split(jax.random.key(seed), 13)
    argo_value = normal_values(keys[0], (TOTAL_OBS, 2 * K), 1.0, 6.0, ((0, 128),), jnp.float32)
    argo_owner_keys = jax.random.split(jax.random.fold_in(keys[1], 1), TOTAL_OBS // OBS_DEV)
    argo_owner_turns = jax.random.permutation(jax.random.fold_in(keys[1], 3), TOTAL_OBS // OBS_DEV)
    argo_owner = jax.vmap(lambda own, number: assign_block(jax.random.fold_in(keys[1], 2), own, number, OBS_DEV, DEVICES, 1, CAP, 2))(argo_owner_keys, argo_owner_turns).reshape((TOTAL_OBS, 1))
    argo_cell = plant(jax.random.randint(keys[2], (TOTAL_OBS,), 0, CJ * CI), jax.random.fold_in(keys[2], 1), 0, (CJ * CI) - 1).astype(jnp.int32)
    alt_value = normal_values(keys[3], (TOTAL_ALT,), 1.0, 6.0, ((0, 128),), jnp.float32)
    alt_owner_keys = jax.random.split(jax.random.fold_in(keys[4], 1), TOTAL_ALT // ALT_DEV)
    alt_owner_turns = jax.random.permutation(jax.random.fold_in(keys[4], 3), TOTAL_ALT // ALT_DEV)
    alt_owner = jax.vmap(lambda own, number: assign_block(jax.random.fold_in(keys[4], 2), own, number, ALT_DEV, DEVICES, 1, CAPH, 2))(alt_owner_keys, alt_owner_turns).reshape((TOTAL_ALT, 1))
    alt_cell = plant(jax.random.randint(keys[5], (TOTAL_ALT,), 0, CJ * CI), jax.random.fold_in(keys[5], 1), 0, (CJ * CI) - 1).astype(jnp.int32)
    alt_profile = normal_values(keys[6], (2 * K,), 0.5, 3.0, (), jnp.float32)
    land_mask = plant((jax.random.randint(keys[7], (NJ, NI), 0, 4) < 3).astype(jnp.int32), jax.random.fold_in(keys[7], 1), 0, 1)
    coef_east = jnp.clip(0.05 + 0.19 * jax.random.uniform(keys[8], (NJ, NI), jnp.float32) ** levels(keys[8], (NJ, NI), ((0, 32), (1, 4)), -0.2, 0.2), 0.05, 0.24)
    coef_north = jnp.clip(0.05 + 0.19 * jax.random.uniform(keys[9], (NJ, NI), jnp.float32) ** levels(keys[9], (NJ, NI), ((0, 32), (1, 4)), -0.2, 0.2), 0.05, 0.24)
    mirror = draw_mirror(jax.random.fold_in(keys[12], 71), 0)
    vinv = draw_vinv(jax.random.fold_in(keys[12], 71), 0)
    return {"argo_value": argo_value, "argo_owner": argo_owner, "argo_cell": argo_cell, "alt_value": alt_value, "alt_owner": alt_owner, "alt_cell": alt_cell, "alt_profile": alt_profile, "land_mask": land_mask, "coef_east": coef_east, "coef_north": coef_north, "mirror": mirror, "vinv": vinv}


def grid_place(owner_list, cell_list):
    target = owner_list[:, 0]
    row_index = (target // N_IA) * CJ + cell_list // CI
    col_index = (target % N_IA) * CI + cell_list % CI
    return row_index, col_index


def reference(argo_value, argo_owner, argo_cell, alt_value, alt_owner, alt_cell, alt_profile, land_mask, coef_east, coef_north, mirror, vinv):
    row_index, col_index = grid_place(argo_owner, argo_cell)
    forcing = jnp.zeros((2 * K, NJ, NI), jnp.float32).at[:, row_index, col_index].add(argo_value.T)
    alt_rows, alt_cols = grid_place(alt_owner, alt_cell)
    sea_level = jnp.zeros((NJ, NI), jnp.float32).at[alt_rows, alt_cols].add(alt_value)
    state_field = forcing + alt_profile[:, None, None] * sea_level[None]
    wet = land_mask.astype(jnp.float32)
    east_w = coef_east * wet * jnp.roll(wet, -1, 1)
    west_w = jnp.roll(east_w, 1, 1)
    north_w = jnp.concatenate([coef_north[:-1] * wet[:-1] * wet[1:], jnp.zeros((1, NI), jnp.float32)], 0)
    south_w = jnp.concatenate([jnp.zeros((1, NI), jnp.float32), north_w[:-1]], 0)
    fold_w = 0.5 * (coef_north[-1] + coef_north[-1][mirror]) * wet[-1] * wet[-1][mirror]

    def horizontal(level_plane):
        result = level_plane + east_w * (jnp.roll(level_plane, -1, 1) - level_plane) + west_w * (jnp.roll(level_plane, 1, 1) - level_plane)
        upward = jnp.concatenate([level_plane[1:], level_plane[-1:]], 0)
        downward = jnp.concatenate([level_plane[:1], level_plane[:-1]], 0)
        result = result + north_w * (upward - level_plane) + south_w * (downward - level_plane)
        top_term = fold_w * (level_plane[-1][mirror] - level_plane[-1])
        return result.at[-1].add(top_term)

    for sweep in range(ITERS):
        state_field = lax.map(horizontal, state_field)
        field_parts = state_field.reshape(2, K, NJ, NI)
        mixed = [jnp.einsum("jlk,lji->kji", vinv[:, which], field_parts[which], precision=lax.Precision.HIGHEST) for which in range(2)]
        state_field = jnp.stack(mixed).reshape(2 * K, NJ, NI)
    return state_field * wet[None]
```

```python
import jax
import jax.numpy as jnp
from jax import lax
from jax.sharding import PartitionSpec as P

ITERS = 3


def with_halo(cells, sides, width):
    for axis, dim in sides:
        count = lax.axis_size(axis)
        head = lax.slice_in_dim(cells, 0, width, axis=dim)
        tail = lax.slice_in_dim(cells, cells.shape[dim] - width, cells.shape[dim], axis=dim)
        cells = jnp.concatenate(
            [
                lax.ppermute(tail, axis, [(i, (i + 1) % count) for i in range(count)]),
                cells,
                lax.ppermute(head, axis, [((i + 1) % count, i) for i in range(count)]),
            ],
            axis=dim,
        )
    return cells


def partner_2(array, axis, bit):
    return lax.ppermute(array, axis, [(i, i ^ 1 << bit) for i in range(lax.axis_size(axis))])


def split3(x):
    hi = lax.reduce_precision(x, exponent_bits=8, mantissa_bits=7)
    rest = x - hi
    mid = lax.reduce_precision(rest, exponent_bits=8, mantissa_bits=7)
    lo = rest - mid
    return [part.astype(jnp.bfloat16) for part in (hi, mid, lo)]


def onehot_dot(onehot, x):
    width = x.shape[1]
    parts = jnp.concatenate(split3(x), axis=1)
    prod = jnp.dot(onehot.astype(jnp.bfloat16), parts, preferred_element_type=jnp.float32)
    return prod[:, :width] + prod[:, width : 2 * width] + prod[:, 2 * width :]


def slot_onehot(owner_list, devices, capacity):
    target = owner_list[:, 0]
    onehot = (target[:, None] == jnp.arange(devices, dtype=jnp.int32)[None, :]).astype(jnp.int32)
    slot_rank = jnp.sum(jnp.cumsum(onehot, 0) * onehot, 1) - 1
    slot = target * capacity + slot_rank
    return slot[None, :] == jnp.arange(devices * capacity, dtype=jnp.int32)[:, None]


def cell_tables(where, row_count, col_count):
    row_of = where // col_count
    col_of = where % col_count
    row_hot = (row_of[:, None] == jnp.arange(row_count, dtype=jnp.int32)[None, :]).astype(
        jnp.float32
    )
    col_hot = (col_of[:, None] == jnp.arange(col_count, dtype=jnp.int32)[None, :]).astype(
        jnp.float32
    )
    return (row_hot, col_hot)


def body(
    argo_value,
    argo_owner,
    argo_cell,
    alt_value,
    alt_owner,
    alt_cell,
    alt_profile,
    land_mask,
    coef_east,
    coef_north,
    mirror,
    vinv,
):
    row_count, col_count = land_mask.shape
    two_levels = argo_value.shape[1]
    levels = two_levels // 2
    count_ja = lax.axis_size("ja")
    count_ia = lax.axis_size("ia")
    devices = count_ja * count_ia
    cap_argo = max(2, 3 * argo_value.shape[0] // devices)
    argo_rows = jnp.concatenate([argo_value, argo_cell[:, None].astype(jnp.float32)], 1)
    argo_send = onehot_dot(slot_onehot(argo_owner, devices, cap_argo), argo_rows)
    alt_rows = jnp.stack([alt_value, alt_cell.astype(jnp.float32)], 1)
    alt_send = onehot_dot(slot_onehot(alt_owner, devices, cap_argo), alt_rows)
    send = jnp.concatenate([argo_send, alt_send], 1).reshape(devices, cap_argo, two_levels + 3)
    received = lax.all_to_all(send, ("ja", "ia"), split_axis=0, concat_axis=0, tiled=True)
    received = received.reshape(devices * cap_argo, two_levels + 3)
    argo_recv = received[:, :two_levels]
    argo_where = jnp.round(received[:, two_levels]).astype(jnp.int32)
    alt_recv = received[:, two_levels + 1]
    alt_where = jnp.round(received[:, two_levels + 2]).astype(jnp.int32)
    argo_rowhot, argo_colhot = cell_tables(argo_where, row_count, col_count)
    weighted = argo_rowhot.T[:, :, None] * argo_recv[None, :, :]
    forcing = jnp.einsum("jnl,ni->jli", weighted, argo_colhot, precision=lax.Precision.HIGHEST)
    alt_rowhot, alt_colhot = cell_tables(alt_where, row_count, col_count)
    sea_level = jnp.einsum(
        "nj,ni->ji", alt_rowhot * alt_recv[:, None], alt_colhot, precision=lax.Precision.HIGHEST
    )
    state_field = forcing + alt_profile[None, :, None] * sea_level[:, None, :]
    wet = land_mask.astype(jnp.float32)
    coast = with_halo(jnp.stack([wet, coef_east, coef_north]), (("ja", 1), ("ia", 2)), 1)
    wet_pad = coast[0]
    east_pad = coast[1]
    north_pad = coast[2]
    ja_index = lax.axis_index("ja")
    row_index = ja_index * row_count + jnp.arange(row_count, dtype=jnp.int32)
    total_rows = row_count * count_ja
    not_top = (row_index != total_rows - 1).astype(jnp.float32)[:, None]
    not_bottom = (row_index != 0).astype(jnp.float32)[:, None]
    east_w = (east_pad[1:-1, 1:-1] * wet_pad[1:-1, 1:-1] * wet_pad[1:-1, 2:])[:, None, :]
    west_w = (east_pad[1:-1, :-2] * wet_pad[1:-1, :-2] * wet_pad[1:-1, 1:-1])[:, None, :]
    north_w = (north_pad[1:-1, 1:-1] * wet_pad[1:-1, 1:-1] * wet_pad[2:, 1:-1] * not_top)[
        :, None, :
    ]
    south_w = (north_pad[:-2, 1:-1] * wet_pad[:-2, 1:-1] * wet_pad[1:-1, 1:-1] * not_bottom)[
        :, None, :
    ]
    top_device = (ja_index == count_ja - 1).astype(jnp.float32)
    top_select = (jnp.arange(row_count) == row_count - 1).astype(jnp.float32)[:, None, None]
    bit_count = count_ia.bit_length() - 1
    fold_index = mirror - (count_ia - 1 - lax.axis_index("ia")) * col_count
    for sweep in range(ITERS):
        padded = with_halo(state_field, (("ja", 0), ("ia", 2)), 1)
        center = state_field
        updated = (
            center
            + east_w * (padded[1:-1, :, 2:] - center)
            + west_w * (padded[1:-1, :, :-2] - center)
        )
        updated = (
            updated
            + north_w * (padded[2:, :, 1:-1] - center)
            + south_w * (padded[:-2, :, 1:-1] - center)
        )
        top_state = state_field[row_count - 1]
        whole_rows = jnp.concatenate(
            [top_state, wet[row_count - 1][None], coef_north[row_count - 1][None]], 0
        )
        for bit_pos in range(bit_count):
            whole_rows = partner_2(whole_rows, "ia", bit_pos)
        partner = jnp.take(whole_rows, fold_index, axis=1)
        fold_w = (
            0.5
            * (coef_north[row_count - 1] + partner[two_levels + 1])
            * wet[row_count - 1]
            * partner[two_levels]
            * top_device
        )
        partner_state = partner[:two_levels]
        fold_add = fold_w[None] * (partner_state - top_state)
        updated = updated + top_select * fold_add[None, :, :]
        field_parts = updated.reshape(row_count, 2, levels, col_count)
        state_field = jnp.einsum(
            "jclk,jcli->jcki", vinv, field_parts, precision=lax.Precision.HIGHEST
        ).reshape(row_count, two_levels, col_count)
    return jnp.transpose(state_field * wet[:, None, :], (1, 0, 2))


def solution(mesh):
    in_specs = (
        P(("ja", "ia"), None),
        P(("ja", "ia"), None),
        P(("ja", "ia")),
        P(("ja", "ia")),
        P(("ja", "ia"), None),
        P(("ja", "ia")),
        P(),
        P("ja", "ia"),
        P("ja", "ia"),
        P("ja", "ia"),
        P("ia"),
        P("ja", None, None, None),
    )
    out_specs = P(None, "ja", "ia")
    return jax.shard_map(body, mesh=mesh, in_specs=in_specs, out_specs=out_specs, check_vma=False)
```

```python
import jax
import jax.numpy as jnp
from jax import lax
from jax.experimental import pallas as pl
from jax.experimental.pallas import tpu as pltpu
from jax.sharding import PartitionSpec as P

ITERS = 3


def with_halo(cells, sides, width):
    for axis, dim in sides:
        count = lax.axis_size(axis)
        head = lax.slice_in_dim(cells, 0, width, axis=dim)
        tail = lax.slice_in_dim(cells, cells.shape[dim] - width, cells.shape[dim], axis=dim)
        cells = jnp.concatenate(
            [
                lax.ppermute(tail, axis, [(i, (i + 1) % count) for i in range(count)]),
                cells,
                lax.ppermute(head, axis, [((i + 1) % count, i) for i in range(count)]),
            ],
            axis=dim,
        )
    return cells


def split3(x):
    hi = lax.reduce_precision(x, exponent_bits=8, mantissa_bits=7)
    rest = x - hi
    mid = lax.reduce_precision(rest, exponent_bits=8, mantissa_bits=7)
    lo = rest - mid
    return [part.astype(jnp.bfloat16) for part in (hi, mid, lo)]


def onehot_dot(onehot, x):
    width = x.shape[1]
    parts = jnp.concatenate(split3(x), axis=1)
    prod = jnp.dot(onehot.astype(jnp.bfloat16), parts, preferred_element_type=jnp.float32)
    return prod[:, :width] + prod[:, width : 2 * width] + prod[:, 2 * width :]


def slot_onehot(owner_list, devices, capacity):
    target = owner_list[:, 0]
    onehot = (target[:, None] == jnp.arange(devices, dtype=jnp.int32)[None, :]).astype(jnp.int32)
    slot_rank = jnp.sum(jnp.cumsum(onehot, 0) * onehot, 1) - 1
    slot = target * capacity + slot_rank
    return slot[None, :] == jnp.arange(devices * capacity, dtype=jnp.int32)[:, None]


def cell_tables(where, row_count, col_count):
    row_of = where // col_count
    col_of = where % col_count
    row_hot = (row_of[:, None] == jnp.arange(row_count, dtype=jnp.int32)[None, :]).astype(
        jnp.float32
    )
    col_hot = (col_of[:, None] == jnp.arange(col_count, dtype=jnp.int32)[None, :]).astype(
        jnp.float32
    )
    return (row_hot, col_hot)


def body(
    argo_value,
    argo_owner,
    argo_cell,
    alt_value,
    alt_owner,
    alt_cell,
    alt_profile,
    land_mask,
    coef_east,
    coef_north,
    mirror,
    vinv,
):
    row_count, col_count = land_mask.shape
    two_levels = argo_value.shape[1]
    levels = two_levels // 2
    count_ja = lax.axis_size("ja")
    count_ia = lax.axis_size("ia")
    devices = count_ja * count_ia
    cap_argo = max(2, 3 * argo_value.shape[0] // devices)
    argo_rows = jnp.concatenate([argo_value, argo_cell[:, None].astype(jnp.float32)], 1)
    argo_send = onehot_dot(slot_onehot(argo_owner, devices, cap_argo), argo_rows)
    alt_rows = jnp.stack([alt_value, alt_cell.astype(jnp.float32)], 1)
    alt_send = onehot_dot(slot_onehot(alt_owner, devices, cap_argo), alt_rows)
    send = jnp.concatenate([argo_send, alt_send], 1).reshape(devices, cap_argo, two_levels + 3)
    received = lax.all_to_all(send, ("ja", "ia"), split_axis=0, concat_axis=0, tiled=True)
    received = received.reshape(devices * cap_argo, two_levels + 3)
    argo_recv = received[:, :two_levels]
    argo_where = jnp.round(received[:, two_levels]).astype(jnp.int32)
    alt_recv = received[:, two_levels + 1]
    alt_where = jnp.round(received[:, two_levels + 2]).astype(jnp.int32)
    argo_rowhot, argo_colhot = cell_tables(argo_where, row_count, col_count)
    weighted = argo_rowhot.T[:, :, None] * argo_recv[None, :, :]
    forcing = jnp.einsum("jnl,ni->jli", weighted, argo_colhot, precision=lax.Precision.HIGHEST)
    alt_rowhot, alt_colhot = cell_tables(alt_where, row_count, col_count)
    sea_level = jnp.einsum(
        "nj,ni->ji", alt_rowhot * alt_recv[:, None], alt_colhot, precision=lax.Precision.HIGHEST
    )
    state_field = forcing + alt_profile[None, :, None] * sea_level[:, None, :]
    wet = land_mask.astype(jnp.float32)
    coast = with_halo(jnp.stack([wet, coef_east, coef_north]), (("ja", 1), ("ia", 2)), 1)
    wet_pad = coast[0]
    east_pad = coast[1]
    north_pad = coast[2]
    ja_index = lax.axis_index("ja")
    row_index = ja_index * row_count + jnp.arange(row_count, dtype=jnp.int32)
    total_rows = row_count * count_ja
    not_top = (row_index != total_rows - 1).astype(jnp.float32)[:, None]
    not_bottom = (row_index != 0).astype(jnp.float32)[:, None]
    east_w = (east_pad[1:-1, 1:-1] * wet_pad[1:-1, 1:-1] * wet_pad[1:-1, 2:])[:, None, :]
    west_w = (east_pad[1:-1, :-2] * wet_pad[1:-1, :-2] * wet_pad[1:-1, 1:-1])[:, None, :]
    north_w = (north_pad[1:-1, 1:-1] * wet_pad[1:-1, 1:-1] * wet_pad[2:, 1:-1] * not_top)[
        :, None, :
    ]
    south_w = (north_pad[:-2, 1:-1] * wet_pad[:-2, 1:-1] * wet_pad[1:-1, 1:-1] * not_bottom)[
        :, None, :
    ]
    top_device = (ja_index == count_ja - 1).astype(jnp.float32)
    fold_index = mirror - (count_ia - 1 - lax.axis_index("ia")) * col_count
    top_coast = jnp.stack([wet[row_count - 1], coef_north[row_count - 1]])
    top_coast = lax.ppermute(top_coast, "ia", mirror_pairs(count_ia))
    top_coast = jnp.take(top_coast, fold_index, axis=1)
    fold_w = (
        0.5 * (coef_north[row_count - 1] + top_coast[1]) * wet[row_count - 1] * top_coast[0] * top_device
    )
    fold_rows = jnp.zeros((row_count, col_count), jnp.float32).at[row_count - 1].set(fold_w)
    weights = jnp.stack(
        [east_w[:, 0], west_w[:, 0], north_w[:, 0], south_w[:, 0], fold_rows] + [fold_rows * 0.0] * 3,
        axis=1,
    )
    blocks = jnp.zeros((row_count, two_levels, two_levels), jnp.float32)
    blocks = blocks.at[:, :levels, :levels].set(jnp.swapaxes(vinv[:, 0], 1, 2))
    blocks = blocks.at[:, levels:, levels:].set(jnp.swapaxes(vinv[:, 1], 1, 2))
    for sweep in range(ITERS):
        north_halo = lax.ppermute(state_field[0], "ja", [((i + 1) % count_ja, i) for i in range(count_ja)])
        south_halo = lax.ppermute(
            state_field[row_count - 1], "ja", [(i, (i + 1) % count_ja) for i in range(count_ja)]
        )
        east_halo = lax.ppermute(
            state_field[:, :, :1], "ia", [((i + 1) % count_ia, i) for i in range(count_ia)]
        )
        west_halo = lax.ppermute(
            state_field[:, :, col_count - 1 :], "ia", [(i, (i + 1) % count_ia) for i in range(count_ia)]
        )
        partner = lax.ppermute(state_field[row_count - 1], "ia", mirror_pairs(count_ia))
        partner = jnp.take(partner, fold_index, axis=1)
        state_field = sweep_call(
            state_field, north_halo, south_halo, east_halo, west_halo, partner, weights, blocks
        )
    return jnp.transpose(state_field * wet[:, None, :], (1, 0, 2))


def mirror_pairs(count):
    return [(i, count - 1 - i) for i in range(count)]


def sweep_kernel(s_ref, n_ref, so_ref, e_ref, w_ref, p_ref, wt_ref, b_ref, o_ref):
    rows, _, cols = s_ref.shape
    lane = lax.broadcasted_iota(jnp.int32, (1, cols), 1)

    def row_step(j, carry):
        f = s_ref[j]
        up = jnp.where(j == rows - 1, n_ref[...], s_ref[jnp.minimum(j + 1, rows - 1)])
        down = jnp.where(j == 0, so_ref[...], s_ref[jnp.maximum(j - 1, 0)])
        east = jnp.where(lane == cols - 1, e_ref[j], pltpu.roll(f, cols - 1, 1))
        west = jnp.where(lane == 0, w_ref[j], pltpu.roll(f, 1, 1))
        wt = wt_ref[j]
        upd = f + wt[0:1] * (east - f) + wt[1:2] * (west - f)
        upd = upd + wt[2:3] * (up - f) + wt[3:4] * (down - f)
        upd = upd + wt[4:5] * (p_ref[...] - f)
        o_ref[j] = jnp.dot(
            b_ref[j], upd, precision=lax.Precision.HIGHEST, preferred_element_type=jnp.float32
        )
        return carry

    lax.fori_loop(0, rows, row_step, 0)


def sweep_call(state, north, south, east, west, partner, weights, blocks):
    rows, depth, cols = state.shape
    whole = pl.BlockSpec(memory_space=pltpu.VMEM)
    return pl.pallas_call(
        sweep_kernel,
        out_shape=jax.ShapeDtypeStruct(state.shape, jnp.float32),
        in_specs=[whole] * 8,
        out_specs=whole,
        compiler_params=pltpu.CompilerParams(vmem_limit_bytes=48 * 1024 * 1024),
        cost_estimate=pl.CostEstimate(
            flops=2 * rows * depth * depth * cols * 6 + 20 * rows * depth * cols,
            bytes_accessed=2 * state.size * 4 + blocks.size * 4,
            transcendentals=0,
        ),
    )(state, north, south, east, west, partner, weights, blocks)


def solution(mesh):
    in_specs = (
        P(("ja", "ia"), None),
        P(("ja", "ia"), None),
        P(("ja", "ia")),
        P(("ja", "ia")),
        P(("ja", "ia"), None),
        P(("ja", "ia")),
        P(),
        P("ja", "ia"),
        P("ja", "ia"),
        P("ja", "ia"),
        P("ia"),
        P("ja", None, None, None),
    )
    out_specs = P(None, "ja", "ia")
    return jax.shard_map(body, mesh=mesh, in_specs=in_specs, out_specs=out_specs, check_vma=False)
```
